32 devices in a mesh: ri: 16 (over z, y, core), rj: 2 (over x).
Axes of the slice: x: 2, y: 2, z: 4, core: 2. Of those that a mesh axis runs over, the one named last changes fastest.
Arguments:
- pair: bfloat16 [64, 512, 512], P(None, 'ri', 'rj'), may hold values from -6 to 6
- conv1_weight: bfloat16 [3, 3, 64, 64], replicated, may hold values from -0.25 to 0.25
- conv1_bias: float32 [64], replicated, may hold values from -3 to 3
- conv2_weight: bfloat16 [3, 3, 64, 64], replicated, may hold values from -0.25 to 0.25
- conv2_bias: float32 [64], replicated, may hold values from -3 to 3
- head_weight: bfloat16 [64, 37], replicated, may hold values from -60 to 60, as said below
- head_bias: float32 [37], replicated, may hold values from -4 to 4
- bins: int32 [512, 512], P('ri', 'rj'), may hold values from 0 to 36
- mask: int32 [512], replicated, may hold values from 0 to 1, as said below
Outputs:
- grad_pair: bfloat16 [64, 512, 512], P(None, 'ri', 'rj')
- grad_conv1_weight: float32 [3, 3, 64, 64], replicated
- grad_conv1_bias: float32 [64], replicated
- grad_conv2_weight: float32 [3, 3, 64, 64], replicated
- grad_conv2_bias: float32 [64], replicated
- grad_head_weight: float32 [64, 37], replicated
- grad_head_bias: float32 [37], replicated
The draws below stay inside these ranges and needn't reach their ends.
Inputs may be any that keep to these rules, and one draw needn't show every extreme that they name: `mask`: residue 0 is always valid; all valid residues lie before some position that is at least 256. `head_weight`: some bins' weights may reach tens in magnitude, so that logits may reach hundreds.
All inputs are finite; a program needn't handle non-finite values.
Results may differ from the reference program's by a relative error of at most 0.012.
The reference program's roundings to bfloat16 on the way (of `inner_act`, `hidden`, `outer_half` and `inner_half`) count: a program that leaves them out, or rounds other values in their place, can miss the bound.
Values may be sent and summed in bfloat16 or wider, within the bound.
A program may use at most 128 MiB of HBM per device.

```python
import jax
import jax.numpy as jnp
from jax import lax

C = 64
NB = 37
KERNEL_TAPS = 3
DILATION_RATE = 8
L = 512


def draw_head_weight(key, part):
    base_key = jax.random.fold_in(key, 23)
    key_one = jax.random.fold_in(base_key, 0)
    spread_scale = C ** (-0.5)
    result = jnp.clip(jax.random.normal(key_one, (C, NB), jnp.float32), -4.0, 4.0) * spread_scale
    return result.astype(jnp.bfloat16)


def draw_mask(key, part):
    base_key = jax.random.fold_in(key, 11)
    key_length, key_keep = jax.random.split(base_key)
    length_cut = jax.random.randint(key_length, (), L // 2, L + 1)
    keeper = jax.random.randint(key_keep, (L,), 0, 10)
    position = jnp.arange(L, dtype=jnp.int32)
    valid = (position < length_cut) & (keeper > 0) | (position == 0)
    return valid.astype(jnp.int32)


def place_ends(values, rng, least, top_value):
    longest = values.shape.index(max(values.shape))
    spots = []
    for shift in (0, 1):
        where = [jax.random.randint(jax.random.fold_in(rng, axis), (), 0, length) for axis, length in enumerate(values.shape)]
        where[longest] = (where[longest] + shift) % values.shape[longest]
        spots.append(tuple(where))
    return values.at[spots[0]].set(least).at[spots[1]].set(top_value)


def shard_levels(rng, extent, pieces, least, high):
    gain, own = 1.0, jax.random.fold_in(rng, 6)
    for dim, parts in pieces:
        draws = jnp.exp(jax.random.uniform(jax.random.fold_in(own, dim), (parts,), jnp.float32, least / len(pieces), high / len(pieces)))
        gain = gain * jnp.repeat(draws, extent[dim] // parts).reshape([-1 if axis == dim else 1 for axis in range(len(extent))])
    return gain


def scatter_about(rng, extent, deviation, limit, cuts=(), kind=jnp.bfloat16):
    values = deviation * jax.random.normal(rng, extent, jnp.float32)
    if cuts:
        values = values * shard_levels(rng, extent, cuts, -0.22, 0.18)
    return jnp.clip(values, -limit, limit).astype(kind)


def setup_inputs(seed: int = 0) -> dict:
    seeds = jax.random.split(jax.random.key(seed), 10)
    return {
        "pair": scatter_about(seeds[0], (C, L, L), 1.0, 6.0, ((1, 16), (2, 2))),
        "conv1_weight": scatter_about(seeds[1], (KERNEL_TAPS, KERNEL_TAPS, C, C), (KERNEL_TAPS * KERNEL_TAPS * C) ** -0.5, 0.25),
        "conv1_bias": scatter_about(seeds[2], (C,), 0.5, 3.0, (), jnp.float32),
        "conv2_weight": scatter_about(seeds[3], (KERNEL_TAPS, KERNEL_TAPS, C, C), (KERNEL_TAPS * KERNEL_TAPS * C) ** -0.5, 0.25),
        "conv2_bias": scatter_about(seeds[4], (C,), 0.5, 3.0, (), jnp.float32),
        "head_weight": draw_head_weight(jax.random.fold_in(seeds[9], 71), 0),
        "head_bias": scatter_about(seeds[6], (NB,), 1.0, 4.0, (), jnp.float32),
        "bins": place_ends(jax.random.randint(seeds[7], (L, L), 0, NB), jax.random.fold_in(seeds[7], 1), 0, NB - 1).astype(jnp.int32),
        "mask": draw_mask(jax.random.fold_in(seeds[9], 71), 0),
    }


def activate(value):
    return jnp.where(value > 0, value, jnp.expm1(jnp.minimum(value, 0.0)))


def activate_slope(value):
    return jnp.where(value > 0, 1.0, jnp.exp(jnp.minimum(value, 0.0)))


def rounded(value):
    return lax.optimization_barrier(value.astype(jnp.bfloat16))


def padded_input(field):
    border_margin = DILATION_RATE * (KERNEL_TAPS // 2)
    return jnp.pad(field, ((0, 0), (border_margin, border_margin), (border_margin, border_margin)))


def dilated(padded_field, weight):
    return lax.conv_general_dilated(
        padded_field[None].astype(jnp.float32), weight.astype(jnp.float32), (1, 1), [(0, 0), (0, 0)],
        rhs_dilation=(DILATION_RATE, DILATION_RATE), dimension_numbers=("NCHW", "HWIO", "NCHW"),
        precision=lax.Precision.HIGHEST)[0]


def flipped(weight):
    return jnp.transpose(weight[::-1, ::-1], (0, 1, 3, 2))


def tap_sums(padded_field, grad):
    row_extent = grad.shape[1]
    column_extent = grad.shape[2]
    widened_field = padded_field.astype(jnp.float32)
    grad_wide = grad.astype(jnp.float32)
    tap_rows = []
    for row_stride in range(KERNEL_TAPS):
        across = []
        for column_stride in range(KERNEL_TAPS):
            sliding_window = widened_field[:, DILATION_RATE * row_stride:DILATION_RATE * row_stride + row_extent, DILATION_RATE * column_stride:DILATION_RATE * column_stride + column_extent]
            across.append(jnp.einsum("cij,dij->cd", sliding_window, grad_wide, precision=lax.Precision.HIGHEST))
        tap_rows.append(jnp.stack(across))
    return jnp.stack(tap_rows)


def project(weight_wide, field):
    return jnp.einsum("ck,cij->kij", weight_wide, field.astype(jnp.float32), precision=lax.Precision.HIGHEST)


def reference(pair, conv1_weight, conv1_bias, conv2_weight, conv2_bias, head_weight, head_bias, bins, mask):
    valid = mask.astype(jnp.float32)
    pair_mask = valid[:, None] * valid[None, :]
    n_valid = jnp.sum(valid)
    pair_pad = padded_input(pair)
    inner = dilated(pair_pad, conv1_weight) + conv1_bias[:, None, None]
    inner_act = rounded(activate(inner))
    act_pad = padded_input(inner_act)
    outer = dilated(act_pad, conv2_weight) + conv2_bias[:, None, None]
    summed = pair.astype(jnp.float32) + outer
    hidden = rounded(pair_mask[None] * activate(summed))
    mirrored = jnp.transpose(hidden, (0, 2, 1))
    weight_wide = head_weight.astype(jnp.float32)
    logits = 0.5 * (project(weight_wide, hidden) + project(weight_wide, mirrored)) + head_bias[:, None, None]
    peak_logit = jnp.max(logits, axis=0, keepdims=True)
    powered = jnp.exp(logits - peak_logit)
    chance = powered / jnp.sum(powered, axis=0, keepdims=True)
    onehot = (bins[None, :, :] == jnp.arange(NB, dtype=jnp.int32)[:, None, None]).astype(jnp.float32)
    error = pair_mask[None] * (chance - onehot)
    symmetric = 0.5 * (hidden.astype(jnp.float32) + mirrored.astype(jnp.float32))
    grad_head_weight = jnp.einsum("cij,kij->ck", symmetric, error, precision=lax.Precision.HIGHEST) / n_valid
    grad_head_bias = jnp.sum(error, axis=(1, 2)) / n_valid
    slope = jnp.einsum("ck,kij->cij", weight_wide, error, precision=lax.Precision.HIGHEST)
    outer_grad = 0.5 * (slope + jnp.transpose(slope, (0, 2, 1))) * pair_mask[None] * activate_slope(summed)
    outer_half = rounded(outer_grad)
    grad_conv2_weight = tap_sums(act_pad, outer_half) / n_valid
    grad_conv2_bias = jnp.sum(outer_grad, axis=(1, 2)) / n_valid
    inner_grad = dilated(padded_input(outer_half), flipped(conv2_weight)) * activate_slope(inner)
    inner_half = rounded(inner_grad)
    grad_conv1_weight = tap_sums(pair_pad, inner_half) / n_valid
    grad_conv1_bias = jnp.sum(inner_grad, axis=(1, 2)) / n_valid
    grad_pair = (outer_grad + dilated(padded_input(inner_half), flipped(conv1_weight))).astype(jnp.bfloat16)
    return (grad_pair, grad_conv1_weight, grad_conv1_bias, grad_conv2_weight, grad_conv2_bias,
            grad_head_weight, grad_head_bias)
```

```python
import functools

import jax
import jax.numpy as jnp
from jax import lax
from jax.experimental import pallas as pl
from jax.experimental.pallas import tpu as pltpu
from jax.sharding import PartitionSpec as P

KERNEL_TAPS = 3
DILATION_RATE = 8


def with_halo(cells, sides, width):
    for axis, dim in sides:
        count = lax.axis_size(axis)
        ends = count - 1
        head = lax.slice_in_dim(cells, 0, width, axis=dim)
        tail = lax.slice_in_dim(cells, cells.shape[dim] - width, cells.shape[dim], axis=dim)
        cells = jnp.concatenate(
            [
                lax.ppermute(tail, axis, [(i, (i + 1) % count) for i in range(ends)]),
                cells,
                lax.ppermute(head, axis, [((i + 1) % count, i) for i in range(ends)]),
            ],
            axis=dim,
        )
    return cells


def activate(value):
    return jnp.where(value > 0, value, jnp.expm1(jnp.minimum(value, 0.0)))


def activate_slope(value):
    return jnp.where(value > 0, 1.0, jnp.exp(jnp.minimum(value, 0.0)))


def with_rims(residual_block):
    return with_halo(residual_block, (("ri", 1), ("rj", 2)), DILATION_RATE * (KERNEL_TAPS // 2))


def dilated(padded_field, weight):
    return lax.conv_general_dilated(
        padded_field[None],
        weight,
        (1, 1),
        [(0, 0), (0, 0)],
        rhs_dilation=(DILATION_RATE, DILATION_RATE),
        dimension_numbers=("NCHW", "HWIO", "NCHW"),
        preferred_element_type=jnp.float32,
    )[0]


def flipped(weight):
    return jnp.transpose(weight[::-1, ::-1], (0, 1, 3, 2))


def tap_sums(padded_field, grad):
    row_extent = grad.shape[1]
    column_extent = grad.shape[2]
    tap_rows = []
    for row_stride in range(KERNEL_TAPS):
        across = []
        for column_stride in range(KERNEL_TAPS):
            sliding_window = padded_field[
                :,
                DILATION_RATE * row_stride : DILATION_RATE * row_stride + row_extent,
                DILATION_RATE * column_stride : DILATION_RATE * column_stride + column_extent,
            ]
            across.append(
                jnp.einsum("cij,dij->cd", sliding_window, grad, preferred_element_type=jnp.float32)
            )
        tap_rows.append(jnp.stack(across))
    return jnp.stack(tap_rows)


def swap_kernel(count, src, dst, send_sem, recv_sem, own_sem):
    row = lax.axis_index("ri")
    column = lax.axis_index("rj")
    slot = lax.rem(row, count)
    far_column = lax.div(row, count)
    own_group = far_column == column
    barrier = pltpu.get_barrier_semaphore()

    def meets_self(block):
        return jnp.logical_and(own_group, slot == block)

    def exchange(block):
        return pltpu.make_async_remote_copy(
            src_ref=src.at[block],
            dst_ref=dst.at[slot],
            send_sem=send_sem.at[block],
            recv_sem=recv_sem.at[slot],
            device_id=(count * column + block, far_column),
            device_id_type=pl.DeviceIdType.MESH,
        )

    def arrival(block):
        return pltpu.make_async_remote_copy(
            src_ref=src.at[block],
            dst_ref=dst.at[block],
            send_sem=send_sem.at[block],
            recv_sem=recv_sem.at[block],
            device_id=(count * column + block, far_column),
            device_id_type=pl.DeviceIdType.MESH,
        )

    for block in range(count):

        @pl.when(jnp.logical_not(meets_self(block)))
        def _():
            pl.semaphore_signal(
                barrier,
                inc=1,
                device_id=(count * column + block, far_column),
                device_id_type=pl.DeviceIdType.MESH,
            )

    @pl.when(own_group)
    def _():
        pl.semaphore_wait(barrier, count - 1)

    @pl.when(jnp.logical_not(own_group))
    def _():
        pl.semaphore_wait(barrier, count)

    for block in range(count):

        @pl.when(jnp.logical_not(meets_self(block)))
        def _():
            exchange(block).start()

        @pl.when(meets_self(block))
        def _():
            pltpu.make_async_copy(src.at[block], dst.at[block], own_sem).start()

    for block in range(count):

        @pl.when(jnp.logical_not(meets_self(block)))
        def _():
            arrival(block).wait()

        @pl.when(meets_self(block))
        def _():
            pltpu.make_async_copy(src.at[block], dst.at[block], own_sem).wait()


def swapped(blocks):
    count = blocks.shape[0]
    return pl.pallas_call(
        functools.partial(swap_kernel, count),
        out_shape=jax.ShapeDtypeStruct(blocks.shape, blocks.dtype),
        in_specs=[pl.BlockSpec(memory_space=pl.ANY)],
        out_specs=pl.BlockSpec(memory_space=pl.ANY),
        scratch_shapes=[
            pltpu.SemaphoreType.DMA((count,)),
            pltpu.SemaphoreType.DMA((count,)),
            pltpu.SemaphoreType.DMA,
        ],
        compiler_params=pltpu.CompilerParams(collective_id=0, has_side_effects=True),
    )(blocks)


def mirror(block):
    chan_count, row_count, col_count = block.shape
    count = col_count // row_count
    parts = block.reshape(chan_count, row_count, count, row_count)
    parts = jnp.transpose(parts, (2, 0, 3, 1)).reshape(count, -1, 128)
    arrived = swapped(parts).reshape(count, chan_count, row_count, row_count)
    return jnp.transpose(arrived, (1, 2, 0, 3)).reshape(chan_count, row_count, col_count)


def summed_over_mesh(flat):
    for axis in ("ri", "rj"):
        size = lax.axis_size(axis)
        stride = 1
        while stride < size:
            flat = flat + lax.ppermute(flat, axis, [(i, i ^ stride) for i in range(size)])
            stride *= 2
    return flat


def sum_arrays(arrays):
    flat = jnp.concatenate([a.reshape(-1) for a in arrays])
    used = flat.shape[0]
    flat = jnp.pad(flat, (0, -used % 1024)).reshape(-1, 128)
    flat = summed_over_mesh(flat).reshape(-1)
    outs = []
    start = 0
    for a in arrays:
        outs.append(flat[start : start + a.size].reshape(a.shape))
        start += a.size
    return outs


def on_device(
    pair, conv1_weight, conv1_bias, conv2_weight, conv2_bias, head_weight, head_bias, bins, mask
):
    row_count = pair.shape[1]
    col_count = pair.shape[2]
    row_valid = lax.dynamic_slice_in_dim(mask, lax.axis_index("ri") * row_count, row_count).astype(
        jnp.float32
    )
    col_valid = lax.dynamic_slice_in_dim(mask, lax.axis_index("rj") * col_count, col_count).astype(
        jnp.float32
    )
    pair_mask = row_valid[:, None] * col_valid[None, :]
    n_valid = jnp.sum(mask.astype(jnp.float32))
    pair_pad = with_rims(pair)
    inner = dilated(pair_pad, conv1_weight) + conv1_bias[:, None, None]
    inner_act = activate(inner).astype(jnp.bfloat16)
    act_pad = with_rims(inner_act)
    outer = dilated(act_pad, conv2_weight) + conv2_bias[:, None, None]
    summed = pair.astype(jnp.float32) + outer
    hidden = (pair_mask[None] * activate(summed)).astype(jnp.bfloat16)
    bins_field = bins.astype(jnp.bfloat16)[None]
    swapped_all = mirror(jnp.concatenate([hidden, bins_field], axis=0))
    mirrored = swapped_all[:-1]
    bins_mirrored = swapped_all[-1].astype(jnp.int32)
    logits = 0.5 * (
        jnp.einsum("ck,cij->kij", head_weight, hidden, preferred_element_type=jnp.float32)
        + jnp.einsum("ck,cij->kij", head_weight, mirrored, preferred_element_type=jnp.float32)
    )
    logits = logits + head_bias[:, None, None]
    peak_logit = jnp.max(logits, axis=0, keepdims=True)
    powered = jnp.exp(logits - peak_logit)
    chance = powered / jnp.sum(powered, axis=0, keepdims=True)
    bin_ids = jnp.arange(head_weight.shape[1], dtype=jnp.int32)[:, None, None]
    onehot = (bins[None] == bin_ids).astype(jnp.float32)
    onehot_mirrored = (bins_mirrored[None] == bin_ids).astype(jnp.float32)
    even_error = pair_mask[None] * (chance - 0.5 * (onehot + onehot_mirrored))
    head_term = jnp.einsum(
        "cij,kij->ck",
        hidden.astype(jnp.float32),
        even_error,
        precision=lax.Precision.HIGHEST,
        preferred_element_type=jnp.float32,
    )
    head_bias_term = jnp.sum(even_error, axis=(1, 2))
    half_slope = jnp.einsum(
        "ck,kij->cij",
        head_weight.astype(jnp.float32),
        even_error,
        precision=lax.Precision.HIGHEST,
        preferred_element_type=jnp.float32,
    )
    outer_grad = half_slope * pair_mask[None] * activate_slope(summed)
    outer_half = outer_grad.astype(jnp.bfloat16)
    conv2_term = tap_sums(act_pad, outer_half)
    conv2_bias_term = jnp.sum(outer_grad, axis=(1, 2))
    inner_grad = dilated(with_rims(outer_half), flipped(conv2_weight)) * activate_slope(inner)
    inner_half = inner_grad.astype(jnp.bfloat16)
    conv1_term = tap_sums(pair_pad, inner_half)
    conv1_bias_term = jnp.sum(inner_grad, axis=(1, 2))
    grad_pair = (outer_grad + dilated(with_rims(inner_half), flipped(conv1_weight))).astype(
        jnp.bfloat16
    )
    late = sum_arrays((conv1_term, conv1_bias_term))
    early = sum_arrays((conv2_term, conv2_bias_term, head_term, head_bias_term))
    return (
        grad_pair,
        late[0] / n_valid,
        late[1] / n_valid,
        early[0] / n_valid,
        early[1] / n_valid,
        early[2] / n_valid,
        early[3] / n_valid,
    )


def solution(mesh):
    return jax.shard_map(
        on_device,
        mesh=mesh,
        in_specs=(P(None, "ri", "rj"), P(), P(), P(), P(), P(), P(), P("ri", "rj"), P()),
        out_specs=(P(None, "ri", "rj"), P(), P(), P(), P(), P(), P()),
        check_vma=False,
    )
```

```python
import functools

import jax
import jax.numpy as jnp
from jax import lax
from jax.experimental import pallas as pl
from jax.experimental.pallas import tpu as pltpu
from jax.sharding import PartitionSpec as P

KERNEL_TAPS = 3
DILATION_RATE = 8


def with_halo(cells, sides, width):
    for axis, dim in sides:
        count = lax.axis_size(axis)
        ends = count - 1
        head = lax.slice_in_dim(cells, 0, width, axis=dim)
        tail = lax.slice_in_dim(cells, cells.shape[dim] - width, cells.shape[dim], axis=dim)
        cells = jnp.concatenate(
            [
                lax.ppermute(tail, axis, [(i, (i + 1) % count) for i in range(ends)]),
                cells,
                lax.ppermute(head, axis, [((i + 1) % count, i) for i in range(ends)]),
            ],
            axis=dim,
        )
    return cells


def activate(value):
    return jnp.where(value > 0, value, jnp.expm1(jnp.minimum(value, 0.0)))


def activate_slope(value):
    return jnp.where(value > 0, 1.0, jnp.exp(jnp.minimum(value, 0.0)))


def with_rims(residual_block):
    return with_halo(residual_block, (("ri", 0), ("rj", 2)), DILATION_RATE * (KERNEL_TAPS // 2))


def spread_taps(field, shifted):
    rows, _, cols = shifted.shape
    chans = field.shape[1]

    @pl.loop(0, rows)
    def _(row):
        line = field[row]
        for tap in range(KERNEL_TAPS):
            start = DILATION_RATE * tap
            shifted[row, chans * tap : chans * (tap + 1), :] = line[:, start : start + cols]


def tap_stack(shifted, row):
    return jnp.concatenate(
        [shifted[row + DILATION_RATE * tap] for tap in range(KERNEL_TAPS)], axis=0
    )


def conv_kernel(field, weight, out, shifted):
    spread_taps(field, shifted)

    @pl.loop(0, out.shape[0])
    def _(row):
        out[row] = jnp.dot(
            weight[...], tap_stack(shifted, row), preferred_element_type=jnp.float32
        )


def tap_kernel(field, grad, out, shifted):
    spread_taps(field, shifted)
    out[...] = jnp.zeros_like(out)

    @pl.loop(0, grad.shape[0])
    def _(row):
        out[...] += lax.dot_general(
            tap_stack(shifted, row),
            grad[row],
            (((1,), (1,)), ((), ())),
            preferred_element_type=jnp.float32,
        )


def row_call(kernel, field, other, out_shape):
    rows, chans, cols = field.shape
    margin = DILATION_RATE * (KERNEL_TAPS - 1)
    whole = pl.BlockSpec(memory_space=pltpu.VMEM)
    flops = 2 * (rows - margin) * (cols - margin) * (KERNEL_TAPS * chans) ** 2
    return pl.pallas_call(
        kernel,
        out_shape=jax.ShapeDtypeStruct(out_shape, jnp.float32),
        in_specs=[whole, whole],
        out_specs=whole,
        scratch_shapes=[pltpu.VMEM((rows, KERNEL_TAPS * chans, cols - margin), jnp.bfloat16)],
        cost_estimate=pl.CostEstimate(
            flops=flops, bytes_accessed=4 * rows * chans * cols, transcendentals=0
        ),
        compiler_params=pltpu.CompilerParams(vmem_limit_bytes=40 * 1024 * 1024),
    )(field, other)


def dilated(padded_field, weight):
    rows, chans, cols = padded_field.shape
    margin = DILATION_RATE * (KERNEL_TAPS - 1)
    flat_weight = weight.reshape(-1, weight.shape[-1]).T
    return row_call(
        conv_kernel, padded_field, flat_weight, (rows - margin, flat_weight.shape[0], cols - margin)
    )


def flipped(weight):
    return jnp.transpose(weight[::-1, ::-1], (0, 1, 3, 2))


def tap_sums(padded_field, grad):
    chans = padded_field.shape[1]
    sums = row_call(
        tap_kernel, padded_field, grad, (KERNEL_TAPS * KERNEL_TAPS * chans, grad.shape[1])
    )
    return sums.reshape(KERNEL_TAPS, KERNEL_TAPS, chans, grad.shape[1])


def swap_kernel(count, src, dst, send_sem, recv_sem, own_sem):
    row = lax.axis_index("ri")
    column = lax.axis_index("rj")
    slot = lax.rem(row, count)
    far_column = lax.div(row, count)
    own_group = far_column == column
    barrier = pltpu.get_barrier_semaphore()

    def meets_self(block):
        return jnp.logical_and(own_group, slot == block)

    def exchange(block):
        return pltpu.make_async_remote_copy(
            src_ref=src.at[block],
            dst_ref=dst.at[slot],
            send_sem=send_sem.at[block],
            recv_sem=recv_sem.at[slot],
            device_id=(count * column + block, far_column),
            device_id_type=pl.DeviceIdType.MESH,
        )

    def arrival(block):
        return pltpu.make_async_remote_copy(
            src_ref=src.at[block],
            dst_ref=dst.at[block],
            send_sem=send_sem.at[block],
            recv_sem=recv_sem.at[block],
            device_id=(count * column + block, far_column),
            device_id_type=pl.DeviceIdType.MESH,
        )

    for block in range(count):

        @pl.when(jnp.logical_not(meets_self(block)))
        def _():
            pl.semaphore_signal(
                barrier,
                inc=1,
                device_id=(count * column + block, far_column),
                device_id_type=pl.DeviceIdType.MESH,
            )

    @pl.when(own_group)
    def _():
        pl.semaphore_wait(barrier, count - 1)

    @pl.when(jnp.logical_not(own_group))
    def _():
        pl.semaphore_wait(barrier, count)

    for block in range(count):

        @pl.when(jnp.logical_not(meets_self(block)))
        def _():
            exchange(block).start()

        @pl.when(meets_self(block))
        def _():
            pltpu.make_async_copy(src.at[block], dst.at[block], own_sem).start()

    for block in range(count):

        @pl.when(jnp.logical_not(meets_self(block)))
        def _():
            arrival(block).wait()

        @pl.when(meets_self(block))
        def _():
            pltpu.make_async_copy(src.at[block], dst.at[block], own_sem).wait()


def swapped(blocks):
    count = blocks.shape[0]
    return pl.pallas_call(
        functools.partial(swap_kernel, count),
        out_shape=jax.ShapeDtypeStruct(blocks.shape, blocks.dtype),
        in_specs=[pl.BlockSpec(memory_space=pl.ANY)],
        out_specs=pl.BlockSpec(memory_space=pl.ANY),
        scratch_shapes=[
            pltpu.SemaphoreType.DMA((count,)),
            pltpu.SemaphoreType.DMA((count,)),
            pltpu.SemaphoreType.DMA,
        ],
        compiler_params=pltpu.CompilerParams(collective_id=0, has_side_effects=True),
    )(blocks)


def mirror(block):
    row_count, chan_count, col_count = block.shape
    count = col_count // row_count
    parts = block.reshape(row_count, chan_count, count, row_count)
    parts = jnp.transpose(parts, (2, 3, 1, 0)).reshape(count, -1, 128)
    arrived = swapped(parts).reshape(count, row_count, chan_count, row_count)
    return jnp.transpose(arrived, (1, 2, 0, 3)).reshape(row_count, chan_count, col_count)


def summed_over_mesh(flat):
    for axis in ("ri", "rj"):
        size = lax.axis_size(axis)
        stride = 1
        while stride < size:
            flat = flat + lax.ppermute(flat, axis, [(i, i ^ stride) for i in range(size)])
            stride *= 2
    return flat


def sum_arrays(arrays):
    flat = jnp.concatenate([a.reshape(-1) for a in arrays])
    used = flat.shape[0]
    flat = jnp.pad(flat, (0, -used % 1024)).reshape(-1, 128)
    flat = summed_over_mesh(flat).reshape(-1)
    outs = []
    start = 0
    for a in arrays:
        outs.append(flat[start : start + a.size].reshape(a.shape))
        start += a.size
    return outs


def on_device(
    pair, conv1_weight, conv1_bias, conv2_weight, conv2_bias, head_weight, head_bias, bins, mask
):
    pair = jnp.transpose(pair, (1, 0, 2))
    row_count = pair.shape[0]
    col_count = pair.shape[2]
    row_valid = lax.dynamic_slice_in_dim(mask, lax.axis_index("ri") * row_count, row_count).astype(
        jnp.float32
    )
    col_valid = lax.dynamic_slice_in_dim(mask, lax.axis_index("rj") * col_count, col_count).astype(
        jnp.float32
    )
    pair_mask = row_valid[:, None] * col_valid[None, :]
    n_valid = jnp.sum(mask.astype(jnp.float32))
    pair_pad = with_rims(pair)
    inner = dilated(pair_pad, conv1_weight) + conv1_bias[:, None]
    inner_act = activate(inner).astype(jnp.bfloat16)
    act_pad = with_rims(inner_act)
    outer = dilated(act_pad, conv2_weight) + conv2_bias[:, None]
    summed = pair.astype(jnp.float32) + outer
    hidden = (pair_mask[:, None, :] * activate(summed)).astype(jnp.bfloat16)
    bins_field = bins.astype(jnp.bfloat16)[:, None, :]
    swapped_all = mirror(jnp.concatenate([hidden, bins_field], axis=1))
    mirrored = swapped_all[:, :-1]
    bins_mirrored = swapped_all[:, -1].astype(jnp.int32)
    logits = 0.5 * (
        jnp.einsum("ck,icj->ikj", head_weight, hidden, preferred_element_type=jnp.float32)
        + jnp.einsum("ck,icj->ikj", head_weight, mirrored, preferred_element_type=jnp.float32)
    )
    logits = logits + head_bias[:, None]
    peak_logit = jnp.max(logits, axis=1, keepdims=True)
    powered = jnp.exp(logits - peak_logit)
    chance = powered / jnp.sum(powered, axis=1, keepdims=True)
    bin_ids = jnp.arange(head_weight.shape[1], dtype=jnp.int32)[:, None]
    onehot = (bins[:, None, :] == bin_ids).astype(jnp.float32)
    onehot_mirrored = (bins_mirrored[:, None, :] == bin_ids).astype(jnp.float32)
    even_error = pair_mask[:, None, :] * (chance - 0.5 * (onehot + onehot_mirrored))
    head_term = jnp.einsum(
        "icj,ikj->ck",
        hidden.astype(jnp.float32),
        even_error,
        precision=lax.Precision.HIGHEST,
        preferred_element_type=jnp.float32,
    )
    head_bias_term = jnp.sum(even_error, axis=(0, 2))
    half_slope = jnp.einsum(
        "ck,ikj->icj",
        head_weight.astype(jnp.float32),
        even_error,
        precision=lax.Precision.HIGHEST,
        preferred_element_type=jnp.float32,
    )
    outer_grad = half_slope * pair_mask[:, None, :] * activate_slope(summed)
    outer_half = outer_grad.astype(jnp.bfloat16)
    conv2_term = tap_sums(act_pad, outer_half)
    conv2_bias_term = jnp.sum(outer_grad, axis=(0, 2))
    inner_grad = dilated(with_rims(outer_half), flipped(conv2_weight)) * activate_slope(inner)
    inner_half = inner_grad.astype(jnp.bfloat16)
    conv1_term = tap_sums(pair_pad, inner_half)
    conv1_bias_term = jnp.sum(inner_grad, axis=(0, 2))
    grad_pair = (outer_grad + dilated(with_rims(inner_half), flipped(conv1_weight))).astype(
        jnp.bfloat16
    )
    late = sum_arrays((conv1_term, conv1_bias_term))
    early = sum_arrays((conv2_term, conv2_bias_term, head_term, head_bias_term))
    return (
        jnp.transpose(grad_pair, (1, 0, 2)),
        late[0] / n_valid,
        late[1] / n_valid,
        early[0] / n_valid,
        early[1] / n_valid,
        early[2] / n_valid,
        early[3] / n_valid,
    )


def solution(mesh):
    return jax.shard_map(
        on_device,
        mesh=mesh,
        in_specs=(P(None, "ri", "rj"), P(), P(), P(), P(), P(), P(), P("ri", "rj"), P()),
        out_specs=(P(None, "ri", "rj"), P(), P(), P(), P(), P(), P()),
        check_vma=False,
    )
```

```python
import functools

import jax
import jax.numpy as jnp
from jax import lax
from jax.experimental import pallas as pl
from jax.experimental.pallas import tpu as pltpu
from jax.sharding import PartitionSpec as P

KERNEL_TAPS = 3
DILATION_RATE = 8


def with_halo(cells, sides, width):
    for axis, dim in sides:
        count = lax.axis_size(axis)
        ends = count - 1
        head = lax.slice_in_dim(cells, 0, width, axis=dim)
        tail = lax.slice_in_dim(cells, cells.shape[dim] - width, cells.shape[dim], axis=dim)
        cells = jnp.concatenate(
            [
                lax.ppermute(tail, axis, [(i, (i + 1) % count) for i in range(ends)]),
                cells,
                lax.ppermute(head, axis, [((i + 1) % count, i) for i in range(ends)]),
            ],
            axis=dim,
        )
    return cells


def activate(value):
    return jnp.where(value > 0, value, jnp.expm1(jnp.minimum(value, 0.0)))


def activate_slope(value):
    return jnp.where(value > 0, 1.0, jnp.exp(jnp.minimum(value, 0.0)))


def with_rims(residual_block):
    return with_halo(residual_block, (("ri", 0), ("rj", 2)), DILATION_RATE * (KERNEL_TAPS // 2))


def spread_taps(field, shifted):
    rows, _, cols = shifted.shape
    chans = field.shape[1]

    @pl.loop(0, rows)
    def _(row):
        line = field[row]
        for tap in range(KERNEL_TAPS):
            start = DILATION_RATE * tap
            shifted[row, chans * tap : chans * (tap + 1), :] = line[:, start : start + cols]


def tap_stack(shifted, row):
    return jnp.concatenate(
        [shifted[row + DILATION_RATE * tap] for tap in range(KERNEL_TAPS)], axis=0
    )


def conv_kernel(field, weight, out, shifted):
    spread_taps(field, shifted)

    @pl.loop(0, out.shape[0])
    def _(row):
        out[row] = jnp.dot(
            weight[...], tap_stack(shifted, row), preferred_element_type=jnp.float32
        )


def tap_kernel(field, grad, out, shifted):
    spread_taps(field, shifted)
    out[...] = jnp.zeros_like(out)

    @pl.loop(0, grad.shape[0])
    def _(row):
        out[...] += lax.dot_general(
            tap_stack(shifted, row),
            grad[row],
            (((1,), (1,)), ((), ())),
            preferred_element_type=jnp.float32,
        )


def row_call(kernel, field, other, out_shape):
    rows, chans, cols = field.shape
    margin = DILATION_RATE * (KERNEL_TAPS - 1)
    whole = pl.BlockSpec(memory_space=pltpu.VMEM)
    flops = 2 * (rows - margin) * (cols - margin) * (KERNEL_TAPS * chans) ** 2
    return pl.pallas_call(
        kernel,
        out_shape=jax.ShapeDtypeStruct(out_shape, jnp.float32),
        in_specs=[whole, whole],
        out_specs=whole,
        scratch_shapes=[pltpu.VMEM((rows, KERNEL_TAPS * chans, cols - margin), jnp.bfloat16)],
        cost_estimate=pl.CostEstimate(
            flops=flops, bytes_accessed=4 * rows * chans * cols, transcendentals=0
        ),
        compiler_params=pltpu.CompilerParams(vmem_limit_bytes=40 * 1024 * 1024),
    )(field, other)


def dilated(padded_field, weight):
    rows, chans, cols = padded_field.shape
    margin = DILATION_RATE * (KERNEL_TAPS - 1)
    flat_weight = weight.reshape(-1, weight.shape[-1]).T
    return row_call(
        conv_kernel, padded_field, flat_weight, (rows - margin, flat_weight.shape[0], cols - margin)
    )


def flipped(weight):
    return jnp.transpose(weight[::-1, ::-1], (0, 1, 3, 2))


def tap_sums(padded_field, grad):
    chans = padded_field.shape[1]
    sums = row_call(
        tap_kernel, padded_field, grad, (KERNEL_TAPS * KERNEL_TAPS * chans, grad.shape[1])
    )
    return sums.reshape(KERNEL_TAPS, KERNEL_TAPS, chans, grad.shape[1])


def swap_kernel(count, wide_src, small_src, wide_dst, small_dst, send_sem, recv_sem, own_sem):
    lanes = ((0, wide_src, wide_dst), (1, small_src, small_dst))
    row = lax.axis_index("ri")
    column = lax.axis_index("rj")
    slot = lax.rem(row, count)
    far_column = lax.div(row, count)
    own_group = far_column == column
    barrier = pltpu.get_barrier_semaphore()

    def meets_self(block):
        return jnp.logical_and(own_group, slot == block)

    def exchange(lane, src, dst, block):
        return pltpu.make_async_remote_copy(
            src_ref=src.at[block],
            dst_ref=dst.at[slot],
            send_sem=send_sem.at[lane, block],
            recv_sem=recv_sem.at[lane, slot],
            device_id=(count * column + block, far_column),
            device_id_type=pl.DeviceIdType.MESH,
        )

    def arrival(lane, src, dst, block):
        return pltpu.make_async_remote_copy(
            src_ref=src.at[block],
            dst_ref=dst.at[block],
            send_sem=send_sem.at[lane, block],
            recv_sem=recv_sem.at[lane, block],
            device_id=(count * column + block, far_column),
            device_id_type=pl.DeviceIdType.MESH,
        )

    for block in range(count):

        @pl.when(jnp.logical_not(meets_self(block)))
        def _():
            pl.semaphore_signal(
                barrier,
                inc=1,
                device_id=(count * column + block, far_column),
                device_id_type=pl.DeviceIdType.MESH,
            )

    @pl.when(own_group)
    def _():
        pl.semaphore_wait(barrier, count - 1)

    @pl.when(jnp.logical_not(own_group))
    def _():
        pl.semaphore_wait(barrier, count)

    for block in range(count):

        @pl.when(jnp.logical_not(meets_self(block)))
        def _():
            for part in lanes:
                exchange(*part, block).start()

        @pl.when(meets_self(block))
        def _():
            for lane, src, dst in lanes:
                pltpu.make_async_copy(src.at[block], dst.at[block], own_sem.at[lane]).start()

    for block in range(count):

        @pl.when(jnp.logical_not(meets_self(block)))
        def _():
            for part in lanes:
                arrival(*part, block).wait()

        @pl.when(meets_self(block))
        def _():
            for lane, src, dst in lanes:
                pltpu.make_async_copy(src.at[block], dst.at[block], own_sem.at[lane]).wait()


def swapped(wide, small):
    count = wide.shape[0]
    anywhere = pl.BlockSpec(memory_space=pl.ANY)
    return pl.pallas_call(
        functools.partial(swap_kernel, count),
        out_shape=[jax.ShapeDtypeStruct(a.shape, a.dtype) for a in (wide, small)],
        in_specs=[anywhere, anywhere],
        out_specs=[anywhere, anywhere],
        scratch_shapes=[
            pltpu.SemaphoreType.DMA((2, count)),
            pltpu.SemaphoreType.DMA((2, count)),
            pltpu.SemaphoreType.DMA((2,)),
        ],
        compiler_params=pltpu.CompilerParams(collective_id=0, has_side_effects=True),
    )(wide, small)


def mirror(field, labels):
    rows, chans, cols = field.shape
    count = cols // rows
    half = rows // 2
    wide = jnp.concatenate([field[:half], field[half:]], axis=1)
    wide = jnp.transpose(wide.reshape(half, 2 * chans, count, rows), (2, 3, 0, 1))
    small = jnp.transpose(labels.reshape(rows, count, rows), (1, 2, 0))
    wide, small = swapped(
        wide.reshape(count, rows * half, 2 * chans), small.reshape(count, -1, 128)
    )
    wide = wide.reshape(count, rows, half, 2 * chans)
    wide = jnp.concatenate([wide[..., :chans], wide[..., chans:]], axis=2)
    field = jnp.transpose(wide, (1, 3, 0, 2)).reshape(rows, chans, cols)
    labels = jnp.transpose(small.reshape(count, rows, rows), (1, 0, 2)).reshape(rows, cols)
    return field, labels


def sum_kernel(
    row_axis, column_axis, own, out, slots, middle, whole,
    send_one, recv_one, send_two, recv_two, send_three, recv_three,
):
    row = lax.axis_index("ri")
    column = lax.axis_index("rj")
    barrier = pltpu.get_barrier_semaphore()
    row_peers = [(step, lax.rem(row + step, row_axis)) for step in range(1, row_axis)]
    column_peers = [(step, lax.rem(column + step, column_axis)) for step in range(1, column_axis)]
    for _, peer in row_peers:
        pl.semaphore_signal(
            barrier, inc=1, device_id=(peer, column), device_id_type=pl.DeviceIdType.MESH
        )
    for _, peer in column_peers:
        pl.semaphore_signal(
            barrier, inc=1, device_id=(row, peer), device_id_type=pl.DeviceIdType.MESH
        )
    pl.semaphore_wait(barrier, row_axis + column_axis - 2)

    def exchange(copies):
        for copy in copies:
            copy.start()
        for copy in copies:
            copy.wait()

    exchange(
        [
            pltpu.make_async_remote_copy(
                src_ref=own.at[peer],
                dst_ref=slots.at[step],
                send_sem=send_one.at[step],
                recv_sem=recv_one.at[step],
                device_id=(peer, column),
                device_id_type=pl.DeviceIdType.MESH,
            )
            for step, peer in row_peers
        ]
    )
    total = own[row]
    for step, _ in row_peers:
        total = total + slots[step]
    middle[column] = total
    exchange(
        [
            pltpu.make_async_remote_copy(
                src_ref=middle.at[column],
                dst_ref=middle.at[column],
                send_sem=send_two.at[step],
                recv_sem=recv_two.at[step],
                device_id=(row, peer),
                device_id_type=pl.DeviceIdType.MESH,
            )
            for step, peer in column_peers
        ]
    )
    total = middle[0]
    for index in range(1, column_axis):
        total = total + middle[index]
    whole[row] = total
    exchange(
        [
            pltpu.make_async_remote_copy(
                src_ref=whole.at[row],
                dst_ref=whole.at[row],
                send_sem=send_three.at[step],
                recv_sem=recv_three.at[step],
                device_id=(peer, column),
                device_id_type=pl.DeviceIdType.MESH,
            )
            for step, peer in row_peers
        ]
    )
    out[...] = whole[...]


def summed_over_mesh(blocks):
    row_axis = lax.axis_size("ri")
    column_axis = lax.axis_size("rj")
    in_vmem = pl.BlockSpec(memory_space=pltpu.VMEM)
    return pl.pallas_call(
        functools.partial(sum_kernel, row_axis, column_axis),
        out_shape=jax.ShapeDtypeStruct(blocks.shape, blocks.dtype),
        in_specs=[in_vmem],
        out_specs=in_vmem,
        scratch_shapes=[
            pltpu.VMEM(blocks.shape, blocks.dtype),
            pltpu.VMEM((column_axis,) + blocks.shape[1:], blocks.dtype),
            pltpu.VMEM(blocks.shape, blocks.dtype),
        ]
        + [
            pltpu.SemaphoreType.DMA((size,))
            for size in (row_axis, row_axis, column_axis, column_axis, row_axis, row_axis)
        ],
        compiler_params=pltpu.CompilerParams(collective_id=1, has_side_effects=True),
    )(blocks)


def sum_arrays(arrays):
    flat = jnp.concatenate([a.reshape(-1) for a in arrays])
    parts = lax.axis_size("ri")
    flat = jnp.pad(flat, (0, -flat.shape[0] % (parts * 1024))).reshape(parts, -1, 128)
    flat = summed_over_mesh(flat).reshape(-1)
    outs = []
    start = 0
    for a in arrays:
        outs.append(flat[start : start + a.size].reshape(a.shape))
        start += a.size
    return outs


def on_device(
    pair, conv1_weight, conv1_bias, conv2_weight, conv2_bias, head_weight, head_bias, bins, mask
):
    pair = jnp.transpose(pair, (1, 0, 2))
    row_count = pair.shape[0]
    col_count = pair.shape[2]
    row_valid = lax.dynamic_slice_in_dim(mask, lax.axis_index("ri") * row_count, row_count).astype(
        jnp.float32
    )
    col_valid = lax.dynamic_slice_in_dim(mask, lax.axis_index("rj") * col_count, col_count).astype(
        jnp.float32
    )
    pair_mask = row_valid[:, None] * col_valid[None, :]
    n_valid = jnp.sum(mask.astype(jnp.float32))
    pair_pad = with_rims(pair)
    inner = dilated(pair_pad, conv1_weight) + conv1_bias[:, None]
    inner_act = activate(inner).astype(jnp.bfloat16)
    act_pad = with_rims(inner_act)
    outer = dilated(act_pad, conv2_weight) + conv2_bias[:, None]
    summed = pair.astype(jnp.float32) + outer
    hidden = (pair_mask[:, None, :] * activate(summed)).astype(jnp.bfloat16)
    mirrored, bins_mirrored = mirror(hidden, bins.astype(jnp.bfloat16))
    bins_mirrored = bins_mirrored.astype(jnp.int32)
    logits = 0.5 * (
        jnp.einsum("ck,icj->ikj", head_weight, hidden, preferred_element_type=jnp.float32)
        + jnp.einsum("ck,icj->ikj", head_weight, mirrored, preferred_element_type=jnp.float32)
    )
    logits = logits + head_bias[:, None]
    peak_logit = jnp.max(logits, axis=1, keepdims=True)
    powered = jnp.exp(logits - peak_logit)
    chance = powered / jnp.sum(powered, axis=1, keepdims=True)
    bin_ids = jnp.arange(head_weight.shape[1], dtype=jnp.int32)[:, None]
    onehot = (bins[:, None, :] == bin_ids).astype(jnp.float32)
    onehot_mirrored = (bins_mirrored[:, None, :] == bin_ids).astype(jnp.float32)
    even_error = pair_mask[:, None, :] * (chance - 0.5 * (onehot + onehot_mirrored))
    head_term = jnp.einsum(
        "icj,ikj->ck",
        hidden.astype(jnp.float32),
        even_error,
        precision=lax.Precision.HIGHEST,
        preferred_element_type=jnp.float32,
    )
    head_bias_term = jnp.sum(even_error, axis=(0, 2))
    half_slope = jnp.einsum(
        "ck,ikj->icj",
        head_weight.astype(jnp.float32),
        even_error,
        precision=lax.Precision.HIGHEST,
        preferred_element_type=jnp.float32,
    )
    outer_grad = half_slope * pair_mask[:, None, :] * activate_slope(summed)
    outer_half = outer_grad.astype(jnp.bfloat16)
    conv2_term = tap_sums(act_pad, outer_half)
    conv2_bias_term = jnp.sum(outer_grad, axis=(0, 2))
    inner_grad = dilated(with_rims(outer_half), flipped(conv2_weight)) * activate_slope(inner)
    inner_half = inner_grad.astype(jnp.bfloat16)
    conv1_term = tap_sums(pair_pad, inner_half)
    conv1_bias_term = jnp.sum(inner_grad, axis=(0, 2))
    grad_pair = (outer_grad + dilated(with_rims(inner_half), flipped(conv1_weight))).astype(
        jnp.bfloat16
    )
    totals = sum_arrays(
        (conv1_term, conv1_bias_term, conv2_term, conv2_bias_term, head_term, head_bias_term)
    )
    return (jnp.transpose(grad_pair, (1, 0, 2)), *[total / n_valid for total in totals])


def solution(mesh):
    return jax.shard_map(
        on_device,
        mesh=mesh,
        in_specs=(P(None, "ri", "rj"), P(), P(), P(), P(), P(), P(), P("ri", "rj"), P()),
        out_specs=(P(None, "ri", "rj"), P(), P(), P(), P(), P(), P()),
        check_vma=False,
    )
```

```python
import functools

import jax
import jax.numpy as jnp
from jax import lax
from jax.experimental import pallas as pl
from jax.experimental.pallas import tpu as pltpu
from jax.sharding import PartitionSpec as P

KERNEL_TAPS = 3
DILATION_RATE = 8


def with_halo(cells, sides, width):
    for axis, dim in sides:
        count = lax.axis_size(axis)
        ends = count - 1
        head = lax.slice_in_dim(cells, 0, width, axis=dim)
        tail = lax.slice_in_dim(cells, cells.shape[dim] - width, cells.shape[dim], axis=dim)
        cells = jnp.concatenate(
            [
                lax.ppermute(tail, axis, [(i, (i + 1) % count) for i in range(ends)]),
                cells,
                lax.ppermute(head, axis, [((i + 1) % count, i) for i in range(ends)]),
            ],
            axis=dim,
        )
    return cells


def activate(value):
    return jnp.where(value > 0, value, jnp.expm1(jnp.minimum(value, 0.0)))


def activate_slope(value):
    return jnp.where(value > 0, 1.0, jnp.exp(jnp.minimum(value, 0.0)))


def with_rims(residual_block):
    return with_halo(residual_block, (("ri", 0), ("rj", 2)), DILATION_RATE * (KERNEL_TAPS // 2))


def spread_taps(field, shifted):
    rows, _, cols = shifted.shape
    chans = field.shape[1]

    @pl.loop(0, rows, unroll=4)
    def _(row):
        line = field[row]
        for tap in range(KERNEL_TAPS):
            start = DILATION_RATE * tap
            shifted[row, chans * tap : chans * (tap + 1), :] = line[:, start : start + cols]


def tap_stack(shifted, row):
    return jnp.concatenate(
        [shifted[row + DILATION_RATE * tap] for tap in range(KERNEL_TAPS)], axis=0
    )


def conv_kernel(field, weight, out, shifted):
    spread_taps(field, shifted)

    @pl.loop(0, out.shape[0], unroll=4)
    def _(row):
        out[row] = jnp.dot(
            weight[...], tap_stack(shifted, row), preferred_element_type=jnp.float32
        )


def tap_kernel(field, grad, out, shifted):
    spread_taps(field, shifted)
    out[...] = jnp.zeros_like(out)

    @pl.loop(0, grad.shape[0], unroll=4)
    def _(row):
        out[...] += lax.dot_general(
            tap_stack(shifted, row),
            grad[row],
            (((1,), (1,)), ((), ())),
            preferred_element_type=jnp.float32,
        )


def row_call(kernel, field, other, out_shape):
    rows, chans, cols = field.shape
    margin = DILATION_RATE * (KERNEL_TAPS - 1)
    whole = pl.BlockSpec(memory_space=pltpu.VMEM)
    flops = 2 * (rows - margin) * (cols - margin) * (KERNEL_TAPS * chans) ** 2
    return pl.pallas_call(
        kernel,
        out_shape=jax.ShapeDtypeStruct(out_shape, jnp.float32),
        in_specs=[whole, whole],
        out_specs=whole,
        scratch_shapes=[pltpu.VMEM((rows, KERNEL_TAPS * chans, cols - margin), jnp.bfloat16)],
        cost_estimate=pl.CostEstimate(
            flops=flops, bytes_accessed=4 * rows * chans * cols, transcendentals=0
        ),
        compiler_params=pltpu.CompilerParams(vmem_limit_bytes=40 * 1024 * 1024),
    )(field, other)


def dilated(padded_field, weight):
    rows, chans, cols = padded_field.shape
    margin = DILATION_RATE * (KERNEL_TAPS - 1)
    flat_weight = weight.reshape(-1, weight.shape[-1]).T
    return row_call(
        conv_kernel, padded_field, flat_weight, (rows - margin, flat_weight.shape[0], cols - margin)
    )


def flipped(weight):
    return jnp.transpose(weight[::-1, ::-1], (0, 1, 3, 2))


def tap_sums(padded_field, grad):
    chans = padded_field.shape[1]
    sums = row_call(
        tap_kernel, padded_field, grad, (KERNEL_TAPS * KERNEL_TAPS * chans, grad.shape[1])
    )
    return sums.reshape(KERNEL_TAPS, KERNEL_TAPS, chans, grad.shape[1])


def swap_kernel(count, wide_src, small_src, wide_dst, small_dst, send_sem, recv_sem, own_sem):
    lanes = ((0, wide_src, wide_dst), (1, small_src, small_dst))
    row = lax.axis_index("ri")
    column = lax.axis_index("rj")
    slot = lax.rem(row, count)
    far_column = lax.div(row, count)
    own_group = far_column == column
    barrier = pltpu.get_barrier_semaphore()

    def meets_self(block):
        return jnp.logical_and(own_group, slot == block)

    def exchange(lane, src, dst, block):
        return pltpu.make_async_remote_copy(
            src_ref=src.at[block],
            dst_ref=dst.at[slot],
            send_sem=send_sem.at[lane, block],
            recv_sem=recv_sem.at[lane, slot],
            device_id=(count * column + block, far_column),
            device_id_type=pl.DeviceIdType.MESH,
        )

    def arrival(lane, src, dst, block):
        return pltpu.make_async_remote_copy(
            src_ref=src.at[block],
            dst_ref=dst.at[block],
            send_sem=send_sem.at[lane, block],
            recv_sem=recv_sem.at[lane, block],
            device_id=(count * column + block, far_column),
            device_id_type=pl.DeviceIdType.MESH,
        )

    for block in range(count):

        @pl.when(jnp.logical_not(meets_self(block)))
        def _():
            pl.semaphore_signal(
                barrier,
                inc=1,
                device_id=(count * column + block, far_column),
                device_id_type=pl.DeviceIdType.MESH,
            )

    @pl.when(own_group)
    def _():
        pl.semaphore_wait(barrier, count - 1)

    @pl.when(jnp.logical_not(own_group))
    def _():
        pl.semaphore_wait(barrier, count)

    for block in range(count):

        @pl.when(jnp.logical_not(meets_self(block)))
        def _():
            for part in lanes:
                exchange(*part, block).start()

        @pl.when(meets_self(block))
        def _():
            for lane, src, dst in lanes:
                pltpu.make_async_copy(src.at[block], dst.at[block], own_sem.at[lane]).start()

    for block in range(count):

        @pl.when(jnp.logical_not(meets_self(block)))
        def _():
            for part in lanes:
                arrival(*part, block).wait()

        @pl.when(meets_self(block))
        def _():
            for lane, src, dst in lanes:
                pltpu.make_async_copy(src.at[block], dst.at[block], own_sem.at[lane]).wait()


def swapped(wide, small):
    count = wide.shape[0]
    anywhere = pl.BlockSpec(memory_space=pl.ANY)
    return pl.pallas_call(
        functools.partial(swap_kernel, count),
        out_shape=[jax.ShapeDtypeStruct(a.shape, a.dtype) for a in (wide, small)],
        in_specs=[anywhere, anywhere],
        out_specs=[anywhere, anywhere],
        scratch_shapes=[
            pltpu.SemaphoreType.DMA((2, count)),
            pltpu.SemaphoreType.DMA((2, count)),
            pltpu.SemaphoreType.DMA((2,)),
        ],
        compiler_params=pltpu.CompilerParams(collective_id=0, has_side_effects=True),
    )(wide, small)


def mirror(field, labels):
    rows, chans, cols = field.shape
    count = cols // rows
    half = rows // 2
    wide = jnp.concatenate([field[:half], field[half:]], axis=1)
    wide = jnp.transpose(wide.reshape(half, 2 * chans, count, rows), (2, 3, 0, 1))
    small = jnp.transpose(labels.reshape(rows, count, rows), (1, 2, 0))
    wide, small = swapped(
        wide.reshape(count, rows * half, 2 * chans), small.reshape(count, -1, 128)
    )
    wide = wide.reshape(count, rows, half, 2 * chans)
    wide = jnp.concatenate([wide[..., :chans], wide[..., chans:]], axis=2)
    field = jnp.transpose(wide, (1, 3, 0, 2)).reshape(rows, chans, cols)
    labels = jnp.transpose(small.reshape(count, rows, rows), (1, 0, 2)).reshape(rows, cols)
    return field, labels


def sum_kernel(
    row_axis, column_axis, own, out, slots, middle, whole,
    send_one, recv_one, send_two, recv_two, send_three, recv_three,
):
    row = lax.axis_index("ri")
    column = lax.axis_index("rj")
    barrier = pltpu.get_barrier_semaphore()
    row_peers = [(step, lax.rem(row + step, row_axis)) for step in range(1, row_axis)]
    column_peers = [(step, lax.rem(column + step, column_axis)) for step in range(1, column_axis)]
    for _, peer in row_peers:
        pl.semaphore_signal(
            barrier, inc=1, device_id=(peer, column), device_id_type=pl.DeviceIdType.MESH
        )
    for _, peer in column_peers:
        pl.semaphore_signal(
            barrier, inc=1, device_id=(row, peer), device_id_type=pl.DeviceIdType.MESH
        )
    pl.semaphore_wait(barrier, row_axis + column_axis - 2)

    def exchange(copies):
        for copy in copies:
            copy.start()
        for copy in copies:
            copy.wait()

    exchange(
        [
            pltpu.make_async_remote_copy(
                src_ref=own.at[peer],
                dst_ref=slots.at[step],
                send_sem=send_one.at[step],
                recv_sem=recv_one.at[step],
                device_id=(peer, column),
                device_id_type=pl.DeviceIdType.MESH,
            )
            for step, peer in row_peers
        ]
    )
    total = own[row]
    for step, _ in row_peers:
        total = total + slots[step]
    middle[column] = total
    exchange(
        [
            pltpu.make_async_remote_copy(
                src_ref=middle.at[column],
                dst_ref=middle.at[column],
                send_sem=send_two.at[step],
                recv_sem=recv_two.at[step],
                device_id=(row, peer),
                device_id_type=pl.DeviceIdType.MESH,
            )
            for step, peer in column_peers
        ]
    )
    total = middle[0]
    for index in range(1, column_axis):
        total = total + middle[index]
    whole[row] = total
    exchange(
        [
            pltpu.make_async_remote_copy(
                src_ref=whole.at[row],
                dst_ref=whole.at[row],
                send_sem=send_three.at[step],
                recv_sem=recv_three.at[step],
                device_id=(peer, column),
                device_id_type=pl.DeviceIdType.MESH,
            )
            for step, peer in row_peers
        ]
    )
    out[...] = whole[...]


def summed_over_mesh(blocks):
    row_axis = lax.axis_size("ri")
    column_axis = lax.axis_size("rj")
    in_vmem = pl.BlockSpec(memory_space=pltpu.VMEM)
    return pl.pallas_call(
        functools.partial(sum_kernel, row_axis, column_axis),
        out_shape=jax.ShapeDtypeStruct(blocks.shape, blocks.dtype),
        in_specs=[in_vmem],
        out_specs=in_vmem,
        scratch_shapes=[
            pltpu.VMEM(blocks.shape, blocks.dtype),
            pltpu.VMEM((column_axis,) + blocks.shape[1:], blocks.dtype),
            pltpu.VMEM(blocks.shape, blocks.dtype),
        ]
        + [
            pltpu.SemaphoreType.DMA((size,))
            for size in (row_axis, row_axis, column_axis, column_axis, row_axis, row_axis)
        ],
        compiler_params=pltpu.CompilerParams(collective_id=1, has_side_effects=True),
    )(blocks)


def sum_arrays(arrays):
    flat = jnp.concatenate([a.reshape(-1) for a in arrays])
    parts = lax.axis_size("ri")
    flat = jnp.pad(flat, (0, -flat.shape[0] % (parts * 1024))).reshape(parts, -1, 128)
    flat = summed_over_mesh(flat).reshape(-1)
    outs = []
    start = 0
    for a in arrays:
        outs.append(flat[start : start + a.size].reshape(a.shape))
        start += a.size
    return outs


def on_device(
    pair, conv1_weight, conv1_bias, conv2_weight, conv2_bias, head_weight, head_bias, bins, mask
):
    pair = jnp.transpose(pair, (1, 0, 2))
    row_count = pair.shape[0]
    col_count = pair.shape[2]
    row_valid = lax.dynamic_slice_in_dim(mask, lax.axis_index("ri") * row_count, row_count).astype(
        jnp.float32
    )
    col_valid = lax.dynamic_slice_in_dim(mask, lax.axis_index("rj") * col_count, col_count).astype(
        jnp.float32
    )
    pair_mask = row_valid[:, None] * col_valid[None, :]
    n_valid = jnp.sum(mask.astype(jnp.float32))
    pair_pad = with_rims(pair)
    inner = dilated(pair_pad, conv1_weight) + conv1_bias[:, None]
    inner_act = activate(inner).astype(jnp.bfloat16)
    act_pad = with_rims(inner_act)
    outer = dilated(act_pad, conv2_weight) + conv2_bias[:, None]
    summed = pair.astype(jnp.float32) + outer
    hidden = (pair_mask[:, None, :] * activate(summed)).astype(jnp.bfloat16)
    mirrored, bins_mirrored = mirror(hidden, bins.astype(jnp.bfloat16))
    bins_mirrored = bins_mirrored.astype(jnp.int32)
    logits = 0.5 * (
        jnp.einsum("ck,icj->ikj", head_weight, hidden, preferred_element_type=jnp.float32)
        + jnp.einsum("ck,icj->ikj", head_weight, mirrored, preferred_element_type=jnp.float32)
    )
    logits = logits + head_bias[:, None]
    peak_logit = jnp.max(logits, axis=1, keepdims=True)
    powered = jnp.exp(logits - peak_logit)
    chance = powered / jnp.sum(powered, axis=1, keepdims=True)
    bin_ids = jnp.arange(head_weight.shape[1], dtype=jnp.int32)[:, None]
    onehot = (bins[:, None, :] == bin_ids).astype(jnp.float32)
    onehot_mirrored = (bins_mirrored[:, None, :] == bin_ids).astype(jnp.float32)
    even_error = pair_mask[:, None, :] * (chance - 0.5 * (onehot + onehot_mirrored))
    head_term = jnp.einsum(
        "icj,ikj->ck",
        hidden.astype(jnp.float32),
        even_error,
        precision=lax.Precision.HIGHEST,
        preferred_element_type=jnp.float32,
    )
    head_bias_term = jnp.sum(even_error, axis=(0, 2))
    half_slope = jnp.einsum(
        "ck,ikj->icj",
        head_weight.astype(jnp.float32),
        even_error,
        precision=lax.Precision.HIGHEST,
        preferred_element_type=jnp.float32,
    )
    outer_grad = half_slope * pair_mask[:, None, :] * activate_slope(summed)
    outer_half = outer_grad.astype(jnp.bfloat16)
    conv2_term = tap_sums(act_pad, outer_half)
    conv2_bias_term = jnp.sum(outer_grad, axis=(0, 2))
    inner_grad = dilated(with_rims(outer_half), flipped(conv2_weight)) * activate_slope(inner)
    inner_half = inner_grad.astype(jnp.bfloat16)
    conv1_term = tap_sums(pair_pad, inner_half)
    conv1_bias_term = jnp.sum(inner_grad, axis=(0, 2))
    grad_pair = (outer_grad + dilated(with_rims(inner_half), flipped(conv1_weight))).astype(
        jnp.bfloat16
    )
    totals = sum_arrays(
        (conv1_term, conv1_bias_term, conv2_term, conv2_bias_term, head_term, head_bias_term)
    )
    return (jnp.transpose(grad_pair, (1, 0, 2)), *[total / n_valid for total in totals])


def solution(mesh):
    return jax.shard_map(
        on_device,
        mesh=mesh,
        in_specs=(P(None, "ri", "rj"), P(), P(), P(), P(), P(), P(), P("ri", "rj"), P()),
        out_specs=(P(None, "ri", "rj"), P(), P(), P(), P(), P(), P()),
        check_vma=False,
    )
```
